32 devices in a mesh: dp: 4 (over y, x), center: 8 (over z, core).
Axes of the slice: x: 2, y: 2, z: 4, core: 2. Of those that a mesh axis runs over, the one named last changes fastest.
Arguments:
- embeddings: bfloat16 [1024, 512], P(('dp', 'center')), may hold values from -0.59765625 to 0.59765625
- labels: int32 [1024], P(('dp', 'center')), may hold values from 0 to 1250303, as said below
- centers: bfloat16 [96, 128, 512], P('center'), may hold values from -0.25 to 0.25
- momentum: float32 [96, 128, 512], P('center'), may hold values from -6 to 6
- block_list: int32 [96], P('center'), may hold values from -1 to 9767, as said below
- counts: int32 [8], P('center'), may hold values from 4 to 12, as said below
Outputs:
- loss: float32 [1024], P(('dp', 'center'))
- embed_grad: float32 [1024, 512], P(('dp', 'center'))
- new_centers: bfloat16 [96, 128, 512], P('center')
- new_momentum: float32 [96, 128, 512], P('center')
The draws below stay inside these ranges and needn't reach their ends.
Inputs may be any that keep to these rules, and one draw needn't show every extreme that they name: Center device j has 12 slots; its first counts[j] slots are live and some device has all 12 live. `block_list`: live slot s of center device j holds a block id of j * 1221 to (j + 1) * 1221 - 1, all live ids distinct; every other slot holds -1. The block labels[b] // 128 of every label is held in a live slot.
All inputs are finite; a program needn't handle non-finite values.
Results may differ from the reference program's by a relative error of at most 0.009.
Values may be sent and summed in bfloat16 or wider, within the bound.
No kernel may reach another device: no remote copies, remote signals or barrier semaphores. Data moves between devices by JAX's collectives and lax.ppermute only.
A program may use at most 192 MiB of HBM per device.

```python
import jax
import jax.numpy as jnp
from jax import lax

D = 512
BLK = 128
SLOTS = 12
BLOCKS_DEV = 1221
BATCH = 1024
TILES = 96
N_CENTER = 8


def joint_draw(key):
    base_key = jax.random.fold_in(key, 1234)
    sub_keys = jax.random.split(base_key, 6)
    least_live = (SLOTS + 2) // 3
    counts = jax.random.randint(sub_keys[0], (N_CENTER,), least_live, SLOTS + 1)
    full_rank = jax.random.randint(sub_keys[1], (), 0, N_CENTER)
    counts = jnp.where(jnp.arange(N_CENTER) == full_rank, SLOTS, counts).astype(jnp.int32)
    device_keys = jax.random.split(sub_keys[2], N_CENTER)
    picked = jax.vmap(lambda sub_key: jax.random.permutation(sub_key, BLOCKS_DEV)[:SLOTS])(device_keys)
    block_ids = (picked + jnp.arange(N_CENTER)[:, None] * BLOCKS_DEV).astype(jnp.int32)
    live_mask = jnp.arange(SLOTS)[None, :] < counts[:, None]
    block_list = jnp.where(live_mask, block_ids, -1).reshape(-1).astype(jnp.int32)
    owner_dev = jax.random.randint(sub_keys[3], (BATCH,), 0, N_CENTER)
    raw_draw = jax.random.randint(sub_keys[4], (BATCH,), 0, 1 << 20)
    slot_pick = raw_draw % counts[owner_dev]
    column = jax.random.randint(sub_keys[5], (BATCH,), 0, BLK)
    labels = (block_ids[owner_dev, slot_pick] * BLK + column).astype(jnp.int32)
    return (labels, block_list, counts)


def draw_labels(key, part):
    return joint_draw(key)[0]


def draw_block_list(key, part):
    return joint_draw(key)[1]


def draw_counts(key, part):
    return joint_draw(key)[2]


def shard_levels(key, dims, shards, smallest, high):
    factor_of, own = 1.0, jax.random.fold_in(key, 6)
    for position, shards_of in shards:
        draws = jnp.exp(jax.random.uniform(jax.random.fold_in(own, position), (shards_of,), jnp.float32, smallest / len(shards), high / len(shards)))
        factor_of = factor_of * jnp.repeat(draws, dims[position] // shards_of).reshape([-1 if axis == position else 1 for axis in range(len(dims))])
    return factor_of


def gaussian(key, dims, scale, most, cuts=(), kind=jnp.bfloat16):
    level = shard_levels(key, dims, cuts, -0.22, 0.18) if cuts else 1.0
    drawn = jax.random.normal(key, dims, jnp.float32) * scale * level
    return jnp.minimum(jnp.maximum(drawn, -most), most).astype(kind)


def setup_inputs(seed: int = 0) -> dict:
    seeds = jax.random.split(jax.random.key(seed), 7)
    return {
        "embeddings": gaussian(seeds[0], (BATCH, D), 0.1, 0.59765625, ((0, 32),)),
        "labels": draw_labels(jax.random.fold_in(seeds[6], 71), 0),
        "centers": gaussian(seeds[2], (TILES, BLK, D), D ** -0.5, 0.25, ((0, 8),)),
        "momentum": gaussian(seeds[3], (TILES, BLK, D), 1.0, 6.0, ((0, 8),), jnp.float32),
        "block_list": draw_block_list(jax.random.fold_in(seeds[6], 71), 0),
        "counts": draw_counts(jax.random.fold_in(seeds[6], 71), 0),
    }


logit_scale = 64.0
margin_cos = 0.35
momentum_rate = 0.9
learn_rate = 0.1
tiny_eps = 1e-06

def unit_rows(values):
    squares = lax.optimization_barrier(jnp.sum(values * values, axis=-1, keepdims=True))
    norms = jnp.sqrt(squares + tiny_eps)
    return (values / norms, norms)

def reference(embeddings, labels, centers, momentum, block_list, counts):
    x_float = embeddings.astype(jnp.float32)
    x_unit, x_norm = unit_rows(x_float)
    x_bf = x_unit.astype(jnp.bfloat16)
    label_block = labels // BLK
    label_col = labels % BLK
    col_iota = jnp.arange(BLK, dtype=jnp.int32)
    slot_iota = jnp.arange(SLOTS, dtype=jnp.int32)
    shard_w = centers.reshape(N_CENTER, SLOTS, BLK, D)
    shard_v = momentum.reshape(N_CENTER, SLOTS, BLK, D)
    shard_ids = block_list.reshape(N_CENTER, SLOTS)

    def shard_logits(w_shard, ids_shard, count_one):
        w_float = w_shard.astype(jnp.float32)
        w_unit, w_norm = unit_rows(w_float)
        w_bf = w_unit.astype(jnp.bfloat16).reshape(SLOTS * BLK, D)
        cosine = jnp.dot(x_bf, w_bf.T, preferred_element_type=jnp.float32)
        hit_mask = (ids_shard[None, :, None] == label_block[:, None, None]) & (col_iota[None, None, :] == label_col[:, None, None])
        hit_float = hit_mask.astype(jnp.float32).reshape(BATCH, SLOTS * BLK)
        live_cols = jnp.broadcast_to((slot_iota < count_one)[:, None], (SLOTS, BLK)).reshape(SLOTS * BLK)
        logit = logit_scale * cosine - logit_scale * margin_cos * hit_float
        exp_z = jnp.where(live_cols[None, :], jnp.exp(logit), 0.0)
        return (exp_z, hit_float, logit, w_float, w_unit, w_norm, w_bf)

    def first_pass(inputs):
        w_shard, ids_shard, count_one = inputs
        outs_all = shard_logits(w_shard, ids_shard, count_one)
        exp_z, hit_float, logit = (outs_all[0], outs_all[1], outs_all[2])
        return (lax.optimization_barrier(jnp.sum(exp_z, axis=1)), lax.optimization_barrier(jnp.sum(hit_float * logit, axis=1)))
    part_total, part_pos = lax.map(first_pass, (shard_w, shard_ids, counts))
    total = lax.optimization_barrier(jnp.sum(part_total, axis=0))
    pos_logit = lax.optimization_barrier(jnp.sum(part_pos, axis=0))
    loss = jnp.log(total) - pos_logit

    def second_pass(carry, inputs):
        w_shard, v_shard, ids_shard, count_one = inputs
        exp_z, hit_float, logit, w_float, w_unit, w_norm, w_bf = shard_logits(w_shard, ids_shard, count_one)
        err_bf = (logit_scale * (exp_z / total[:, None] - hit_float)).astype(jnp.bfloat16)
        carry = carry + jnp.dot(err_bf, w_bf, preferred_element_type=jnp.float32)
        grad_unit = lax.dot_general(err_bf, x_bf, (((0,), (0,)), ((), ())), preferred_element_type=jnp.float32).reshape(SLOTS, BLK, D)
        grad_w = (grad_unit - w_unit * lax.optimization_barrier(jnp.sum(w_unit * grad_unit, axis=-1, keepdims=True))) / w_norm
        live_tile = (slot_iota < count_one)[:, None, None]
        v_float = v_shard.astype(jnp.float32)
        new_v = jnp.where(live_tile, momentum_rate * v_float + grad_w, v_float)
        new_w = jnp.where(live_tile, (w_float - learn_rate * new_v).astype(jnp.bfloat16), w_shard)
        return (carry, (new_w, new_v))
    grad_x, (new_w, new_v) = lax.scan(second_pass, jnp.zeros((BATCH, D), jnp.float32), (shard_w, shard_v, shard_ids, counts))
    embed_grad = (grad_x - x_unit * lax.optimization_barrier(jnp.sum(x_unit * grad_x, axis=-1, keepdims=True))) / x_norm
    return (loss, embed_grad, new_w.reshape(TILES, BLK, D), new_v.reshape(TILES, BLK, D))
```

```python
import functools
import math

import jax
import jax.numpy as jnp
from jax import lax
from jax.experimental import pallas as pl
from jax.experimental.pallas import tpu as pltpu
from jax.sharding import PartitionSpec as P

logit_scale = 64.0
margin_cos = 0.35
momentum_rate = 0.9
learn_rate = 0.1
tiny_eps = 1e-06


def unit_rows(values):
    squares = jnp.sum(values * values, axis=-1, keepdims=True)
    norms = jnp.sqrt(squares + tiny_eps)
    return (values / norms, norms)


def update_tiles(grad_unit, w_shard, w_unit, w_norm, v_shard, live_tile):
    grad_w = (grad_unit - w_unit * jnp.sum(w_unit * grad_unit, axis=-1, keepdims=True)) / w_norm
    new_v = jnp.where(live_tile, momentum_rate * v_shard + grad_w, v_shard)
    new_w = jnp.where(
        live_tile, (w_shard.astype(jnp.float32) - learn_rate * new_v).astype(jnp.bfloat16), w_shard
    )
    return (new_w, new_v)


def on_device(embeddings, labels, centers, momentum, block_list, counts):
    rows_dev = embeddings.shape[0]
    slots, blk_size, width = centers.shape
    flat = slots * blk_size
    x_float = embeddings.astype(jnp.float32)
    x_unit, x_norm = unit_rows(x_float)
    x_bf = x_unit.astype(jnp.bfloat16)
    group_x, group_labels = (
        lax.all_gather(x_bf, "center", axis=0, tiled=True),
        lax.all_gather(labels, "center", axis=0, tiled=True),
    )
    group_count = group_x.shape[0]
    w_float = centers.astype(jnp.float32)
    w_unit, w_norm = unit_rows(w_float)
    w_bf = w_unit.astype(jnp.bfloat16).reshape(flat, width)
    slot_iota = jnp.arange(slots, dtype=jnp.int32)
    live_slot = slot_iota < counts[0]
    live_cols = jnp.broadcast_to(live_slot[:, None], (slots, blk_size)).reshape(flat)
    col_iota = jnp.arange(blk_size, dtype=jnp.int32)
    label_block = group_labels // blk_size
    label_col = group_labels % blk_size
    hit_mask = (block_list[None, :, None] == label_block[:, None, None]) & (
        col_iota[None, None, :] == label_col[:, None, None]
    )
    hit_float = hit_mask.astype(jnp.float32).reshape(group_count, flat)
    step_rows = math.gcd(group_count, 512)
    block_total = group_count // step_rows

    def first_pass(inputs):
        x_block, hit_block = inputs
        cosine = lax.dot_general(
            x_block, w_bf, (((1,), (1,)), ((), ())), preferred_element_type=jnp.float32
        )
        logit = logit_scale * cosine - logit_scale * margin_cos * hit_block
        exp_z = jnp.where(live_cols[None, :], jnp.exp(logit), 0.0)
        return (exp_z, jnp.sum(exp_z, axis=1), jnp.sum(hit_block * logit, axis=1))

    exp_z, part_total, part_pos = lax.map(
        first_pass,
        (
            group_x.reshape(block_total, step_rows, width),
            hit_float.reshape(block_total, step_rows, flat),
        ),
    )
    exp_z = exp_z.reshape(group_count, flat)
    total, pos_logit = lax.psum(
        (part_total.reshape(group_count), part_pos.reshape(group_count)), "center"
    )
    my_start = lax.axis_index("center") * rows_dev
    loss = lax.dynamic_slice_in_dim(jnp.log(total) - pos_logit, my_start, rows_dev, 0)
    err_bf = (logit_scale * (exp_z / total[:, None] - hit_float)).astype(jnp.bfloat16)
    grad_x = lax.psum_scatter(
        jnp.dot(err_bf, w_bf, preferred_element_type=jnp.float32),
        "center",
        scatter_dimension=0,
        tiled=True,
    )
    embed_grad = (grad_x - x_unit * jnp.sum(x_unit * grad_x, axis=-1, keepdims=True)) / x_norm
    grad_unit = lax.dot_general(
        err_bf, group_x, (((0,), (0,)), ((), ())), preferred_element_type=jnp.float32
    ).reshape(slots, blk_size, width)
    live_tile = live_slot[:, None, None]
    grad_sum = lax.psum(grad_unit.astype(jnp.bfloat16), "dp").astype(jnp.float32)
    new_w, new_v = update_tiles(grad_sum, centers, w_unit, w_norm, momentum, live_tile)
    return (loss, embed_grad, new_w, new_v)


DIGIT_ROWS = 8
ON_CHIP_BYTES = 24 << 20
KERNEL_VMEM = 24 << 20
VMEM_SPEC = pl.BlockSpec(memory_space=pltpu.VMEM)
SMEM_SPEC = pl.BlockSpec(memory_space=pltpu.SMEM)


def call(kernel, outs, in_specs, scratch=(), flops=0, moved=0):
    return pl.pallas_call(
        kernel,
        out_shape=outs,
        in_specs=in_specs,
        out_specs=jax.tree.map(lambda _: VMEM_SPEC, outs),
        scratch_shapes=scratch,
        compiler_params=pltpu.CompilerParams(vmem_limit_bytes=KERNEL_VMEM),
        cost_estimate=pl.CostEstimate(flops=flops, bytes_accessed=moved, transcendentals=0),
    )


def unit_scale(values):
    return lax.rsqrt(jnp.sum(values * values, axis=-1, keepdims=True) + tiny_eps)


def unit_centers_kernel(centers_ref, unit_ref):
    def step(slot, carry):
        w_float = centers_ref[slot].astype(jnp.float32)
        unit_ref[slot] = (w_float * unit_scale(w_float)).astype(jnp.bfloat16)
        return carry

    lax.fori_loop(0, centers_ref.shape[0], step, 0)


def logits_kernel(
    z_count, rows_dev, chunk, counts_ref, blocks_ref, mine_ref, pair_ref, w_ref,
    x_ref, exp_ref, stat_ref, target_ref, digit_ref,
):
    center = lax.axis_index("center")
    z_own, core = center // 2, center % 2
    piece_rows = rows_dev + DIGIT_ROWS
    pieces = mine_ref.shape[0] // piece_rows
    batch, width = x_ref.shape
    slots = blocks_ref.shape[0]
    flat = w_ref.shape[0]
    blk_size = flat // slots
    for side, source in enumerate((mine_ref, pair_ref)):
        for piece in range(pieces):
            group, z_rel = divmod(piece, z_count)
            place = (group * z_count + (z_own ^ z_rel)) * 2 + (core ^ side)
            base = piece * piece_rows
            x_float = source[base : base + rows_dev, :].astype(jnp.float32)
            start = pl.multiple_of(place * rows_dev, rows_dev)
            x_ref[pl.ds(start, rows_dev), :] = (x_float * unit_scale(x_float)).astype(jnp.bfloat16)
            digit_ref[place] = source[base + rows_dev : base + piece_rows, :128].astype(jnp.float32)
    digits = digit_ref[...].reshape(2 * pieces * DIGIT_ROWS, 128).astype(jnp.bfloat16)
    lane = lax.broadcasted_iota(jnp.int32, (128, batch), 0)
    column = lax.broadcasted_iota(jnp.int32, (128, batch), 1)
    spread = jnp.where(column % rows_dev == lane, 1.0, 0.0).astype(jnp.bfloat16)
    spread_digits = jnp.dot(digits, spread, preferred_element_type=jnp.float32)
    spread_digits = spread_digits.reshape(2 * pieces, DIGIT_ROWS, batch)
    owner = lax.broadcasted_iota(jnp.int32, (DIGIT_ROWS, batch), 1) // rows_dev
    digit_rows = jnp.zeros((DIGIT_ROWS, batch), jnp.float32)
    for place in range(2 * pieces):
        digit_rows = digit_rows + jnp.where(owner == place, spread_digits[place], 0.0)
    digit_ints = digit_rows.astype(jnp.int32)
    label = digit_ints[0:1] + 256 * (digit_ints[1:2] + 256 * (digit_ints[2:3] + 256 * digit_ints[3:4]))
    label_block, label_col = label // blk_size, label % blk_size
    target = jnp.full((1, batch), -1, jnp.int32)
    for slot in range(slots):
        target = jnp.where(label_block == blocks_ref[slot], slot * blk_size + label_col, target)
    target_ref[...] = target
    live_rows = counts_ref[0] * blk_size

    def step(index, carry):
        total, positive = carry
        first = pl.multiple_of(index * chunk, chunk)
        cosine = lax.dot_general(
            w_ref[pl.ds(first, chunk), :], x_ref[...], (((1,), (1,)), ((), ())),
            preferred_element_type=jnp.float32,
        )
        row = lax.broadcasted_iota(jnp.int32, (chunk, batch), 0) + first
        hit = row == target
        logit = logit_scale * cosine
        logit = jnp.where(hit, logit - logit_scale * margin_cos, logit)
        exp_z = jnp.where(row < live_rows, jnp.exp(logit), 0.0)
        exp_ref[pl.ds(first, chunk), :] = exp_z
        positive = positive + jnp.sum(jnp.where(hit, logit, 0.0).reshape(chunk // 8, 8, batch), axis=0)
        total = total + jnp.sum(exp_z.reshape(chunk // 8, 8, batch), axis=0)
        return total, positive

    zeros = jnp.zeros((8, batch), jnp.float32)
    total, positive = lax.fori_loop(0, flat // chunk, step, (zeros, zeros))
    stat_ref[0:1, :] = jnp.sum(total, axis=0, keepdims=True)
    stat_ref[1:2, :] = jnp.sum(positive, axis=0, keepdims=True)


def error_rows(exp_z, first, scale, target):
    row = lax.broadcasted_iota(jnp.int32, exp_z.shape, 0) + first
    scaled = exp_z * scale
    return jnp.where(row == target, scaled - logit_scale, scaled).astype(jnp.bfloat16)


def embed_kernel(z_count, rows_dev, chunk, exp_ref, stat_ref, target_ref, w_ref, out_ref, sum_ref):
    center = lax.axis_index("center")
    z_own, core = center // 2, center % 2
    group_rows = sum_ref.shape[0]
    scale = logit_scale / stat_ref[0:1, :group_rows]
    target = target_ref[0:1, :group_rows]
    sum_ref[...] = jnp.zeros_like(sum_ref)

    def step(index, carry):
        first = pl.multiple_of(index * chunk, chunk)
        err = error_rows(exp_ref[pl.ds(first, chunk), :group_rows], first, scale, target)
        sum_ref[...] += lax.dot_general(
            err, w_ref[pl.ds(first, chunk), :], (((0,), (0,)), ((), ())),
            preferred_element_type=jnp.float32,
        )
        return carry

    lax.fori_loop(0, exp_ref.shape[0] // chunk, step, 0)
    for z_to in range(z_count):
        for core_to in range(2):
            start = (z_to * 2 + core_to) * rows_dev
            out_ref[core ^ core_to, z_own ^ z_to] = sum_ref[start : start + rows_dev, :]


def update_kernel(
    counts_ref, exp_ref, stat_ref, target_ref, x_ref, centers_ref, momentum_ref, new_w_ref, new_v_ref
):
    step_slots, blk_size, width = centers_ref.shape
    first_slot = pl.program_id(0) * step_slots
    rows = step_slots * blk_size
    first = pl.multiple_of(first_slot * blk_size, rows)
    scale = logit_scale / stat_ref[0:1, :]
    err = error_rows(exp_ref[pl.ds(first, rows), :], first, scale, target_ref[...])
    grad_unit = jnp.dot(err, x_ref[...], preferred_element_type=jnp.float32)
    w_float = centers_ref[...].reshape(rows, width).astype(jnp.float32)
    inverse = unit_scale(w_float)
    w_unit = w_float * inverse
    along = jnp.sum(w_unit * grad_unit, axis=-1, keepdims=True)
    grad_w = (grad_unit - w_unit * along) * inverse
    momentum = momentum_ref[...].reshape(rows, width)
    row = lax.broadcasted_iota(jnp.int32, (rows, 1), 0) + first
    live = row < counts_ref[0] * blk_size
    new_v = jnp.where(live, momentum_rate * momentum + grad_w, momentum)
    new_w = jnp.where(live, w_float - learn_rate * new_v, w_float)
    new_v_ref[...] = new_v.reshape(new_v_ref.shape)
    new_w_ref[...] = new_w.astype(jnp.bfloat16).reshape(new_w_ref.shape)


def on_device_permutes(groups, z_count, embeddings, labels, centers, momentum, block_list, counts):
    rows_dev, width = embeddings.shape
    slots, blk_size, _ = centers.shape
    flat = slots * blk_size
    cores = z_count * 2
    batch = groups * cores * rows_dev
    group_rows = cores * rows_dev
    chunk = 2 * blk_size
    axes = ("dp", "center")

    def exchange(array, group_mask, center_mask):
        pairs = [
            (group * cores + center, (group ^ group_mask) * cores + (center ^ center_mask))
            for group in range(groups)
            for center in range(cores)
        ]
        return lax.ppermute(array, axes, pairs)

    digits = jnp.stack([(labels >> shift) & 255 for shift in (0, 8, 16, 24)]).astype(jnp.bfloat16)
    digits = jnp.pad(digits, ((0, DIGIT_ROWS - 4), (0, width - rows_dev)))
    packed = jnp.concatenate([embeddings, digits], axis=0)
    column = jnp.concatenate(
        [packed] + [exchange(packed, 0, 2 * mask) for mask in range(1, z_count)], axis=0
    )
    mine = jnp.concatenate(
        [column] + [exchange(column, mask, 0) for mask in range(1, groups)], axis=0
    )
    pair = exchange(mine, 0, 1)
    w_bf = call(
        unit_centers_kernel,
        jax.ShapeDtypeStruct((slots, blk_size, width), jnp.bfloat16),
        [VMEM_SPEC],
        flops=4 * flat * width,
        moved=4 * flat * width,
    )(centers).reshape(flat, width)
    x_bf, exp_z, stats, target = call(
        functools.partial(logits_kernel, z_count, rows_dev, chunk),
        (
            jax.ShapeDtypeStruct((batch, width), jnp.bfloat16),
            jax.ShapeDtypeStruct((flat, batch), jnp.float32),
            jax.ShapeDtypeStruct((2, batch), jnp.float32),
            jax.ShapeDtypeStruct((1, batch), jnp.int32),
        ),
        [SMEM_SPEC, SMEM_SPEC, VMEM_SPEC, VMEM_SPEC, VMEM_SPEC],
        [pltpu.VMEM((groups * cores, DIGIT_ROWS, 128), jnp.float32)],
        flops=2 * flat * width * batch,
        moved=4 * flat * batch,
    )(counts, block_list, mine, pair, w_bf)
    for mask in (1, *(2 << bit for bit in range(z_count.bit_length() - 1))):
        stats = stats + exchange(stats, 0, mask)
    partial = call(
        functools.partial(embed_kernel, z_count, rows_dev, chunk),
        jax.ShapeDtypeStruct((2, z_count, rows_dev, width), jnp.float32),
        [VMEM_SPEC] * 4,
        [pltpu.VMEM((group_rows, width), jnp.float32)],
        flops=2 * flat * width * group_rows,
        moved=4 * flat * group_rows,
    )(exp_z, stats, target, w_bf)
    chip_sum = partial[0] + exchange(partial[1], 0, 1)
    grad_x = chip_sum[0]
    sent = chip_sum.astype(jnp.bfloat16)
    for mask in range(1, z_count):
        grad_x = grad_x + exchange(sent[mask], 0, 2 * mask).astype(jnp.float32)
    step_slots = math.gcd(slots, 2)
    tile = pl.BlockSpec((step_slots, blk_size, width), lambda step: (step, 0, 0))
    new_w, new_v = pl.pallas_call(
        update_kernel,
        grid=(slots // step_slots,),
        out_shape=(
            jax.ShapeDtypeStruct(centers.shape, centers.dtype),
            jax.ShapeDtypeStruct(momentum.shape, momentum.dtype),
        ),
        in_specs=[SMEM_SPEC, VMEM_SPEC, VMEM_SPEC, VMEM_SPEC, VMEM_SPEC, tile, tile],
        out_specs=(tile, tile),
        compiler_params=pltpu.CompilerParams(vmem_limit_bytes=KERNEL_VMEM),
        cost_estimate=pl.CostEstimate(
            flops=2 * flat * width * batch, bytes_accessed=12 * flat * width, transcendentals=0
        ),
    )(counts, exp_z, stats, target, x_bf, centers, momentum)
    x_float = embeddings.astype(jnp.float32)
    x_unit, x_norm = unit_rows(x_float)
    embed_grad = (grad_x - x_unit * jnp.sum(x_unit * grad_x, axis=-1, keepdims=True)) / x_norm
    my_start = lax.axis_index("center") * rows_dev
    own = lax.dynamic_slice_in_dim(stats, my_start, rows_dev, 1)
    loss = jnp.log(own[0]) - own[1]
    return (loss, embed_grad, new_w, new_v)


def solution(mesh):
    groups, cores = mesh.shape["dp"], mesh.shape["center"]

    def on_mesh(embeddings, labels, centers, momentum, block_list, counts):
        batch, width = embeddings.shape
        tiles, blk_size, _ = centers.shape
        rows_dev = batch // (groups * cores)
        flat = tiles // cores * blk_size
        powers = groups & (groups - 1) == 0 and cores & (cores - 1) == 0 and cores >= 4
        fits = 4 * flat * batch + 8 * batch * width <= ON_CHIP_BYTES
        shapes = rows_dev == 32 and width % 128 == 0 and blk_size == 128
        body = on_device
        if powers and fits and shapes:
            body = functools.partial(on_device_permutes, groups, cores // 2)
        return jax.shard_map(
            body,
            mesh=mesh,
            in_specs=(
                P(("dp", "center"), None),
                P(("dp", "center")),
                P("center", None, None),
                P("center", None, None),
                P("center"),
                P("center"),
            ),
            out_specs=(
                P(("dp", "center")),
                P(("dp", "center"), None),
                P("center", None, None),
                P("center", None, None),
            ),
            check_vma=False,
        )(embeddings, labels, centers, momentum, block_list, counts)

    return on_mesh
```

```python
import functools
import math

import jax
import jax.numpy as jnp
from jax import lax
from jax.experimental import pallas as pl
from jax.experimental.pallas import tpu as pltpu
from jax.sharding import PartitionSpec as P

logit_scale = 64.0
margin_cos = 0.35
momentum_rate = 0.9
learn_rate = 0.1
tiny_eps = 1e-06


def unit_rows(values):
    squares = jnp.sum(values * values, axis=-1, keepdims=True)
    norms = jnp.sqrt(squares + tiny_eps)
    return (values / norms, norms)


def update_tiles(grad_unit, w_shard, w_unit, w_norm, v_shard, live_tile):
    grad_w = (grad_unit - w_unit * jnp.sum(w_unit * grad_unit, axis=-1, keepdims=True)) / w_norm
    new_v = jnp.where(live_tile, momentum_rate * v_shard + grad_w, v_shard)
    new_w = jnp.where(
        live_tile, (w_shard.astype(jnp.float32) - learn_rate * new_v).astype(jnp.bfloat16), w_shard
    )
    return (new_w, new_v)


def on_device(embeddings, labels, centers, momentum, block_list, counts):
    rows_dev = embeddings.shape[0]
    slots, blk_size, width = centers.shape
    flat = slots * blk_size
    x_float = embeddings.astype(jnp.float32)
    x_unit, x_norm = unit_rows(x_float)
    x_bf = x_unit.astype(jnp.bfloat16)
    group_x, group_labels = (
        lax.all_gather(x_bf, "center", axis=0, tiled=True),
        lax.all_gather(labels, "center", axis=0, tiled=True),
    )
    group_count = group_x.shape[0]
    w_float = centers.astype(jnp.float32)
    w_unit, w_norm = unit_rows(w_float)
    w_bf = w_unit.astype(jnp.bfloat16).reshape(flat, width)
    slot_iota = jnp.arange(slots, dtype=jnp.int32)
    live_slot = slot_iota < counts[0]
    live_cols = jnp.broadcast_to(live_slot[:, None], (slots, blk_size)).reshape(flat)
    col_iota = jnp.arange(blk_size, dtype=jnp.int32)
    label_block = group_labels // blk_size
    label_col = group_labels % blk_size
    hit_mask = (block_list[None, :, None] == label_block[:, None, None]) & (
        col_iota[None, None, :] == label_col[:, None, None]
    )
    hit_float = hit_mask.astype(jnp.float32).reshape(group_count, flat)
    step_rows = math.gcd(group_count, 512)
    block_total = group_count // step_rows

    def first_pass(inputs):
        x_block, hit_block = inputs
        cosine = lax.dot_general(
            x_block, w_bf, (((1,), (1,)), ((), ())), preferred_element_type=jnp.float32
        )
        logit = logit_scale * cosine - logit_scale * margin_cos * hit_block
        exp_z = jnp.where(live_cols[None, :], jnp.exp(logit), 0.0)
        return (exp_z, jnp.sum(exp_z, axis=1), jnp.sum(hit_block * logit, axis=1))

    exp_z, part_total, part_pos = lax.map(
        first_pass,
        (
            group_x.reshape(block_total, step_rows, width),
            hit_float.reshape(block_total, step_rows, flat),
        ),
    )
    exp_z = exp_z.reshape(group_count, flat)
    total, pos_logit = lax.psum(
        (part_total.reshape(group_count), part_pos.reshape(group_count)), "center"
    )
    my_start = lax.axis_index("center") * rows_dev
    loss = lax.dynamic_slice_in_dim(jnp.log(total) - pos_logit, my_start, rows_dev, 0)
    err_bf = (logit_scale * (exp_z / total[:, None] - hit_float)).astype(jnp.bfloat16)
    grad_x = lax.psum_scatter(
        jnp.dot(err_bf, w_bf, preferred_element_type=jnp.float32),
        "center",
        scatter_dimension=0,
        tiled=True,
    )
    embed_grad = (grad_x - x_unit * jnp.sum(x_unit * grad_x, axis=-1, keepdims=True)) / x_norm
    grad_unit = lax.dot_general(
        err_bf, group_x, (((0,), (0,)), ((), ())), preferred_element_type=jnp.float32
    ).reshape(slots, blk_size, width)
    live_tile = live_slot[:, None, None]
    grad_sum = lax.psum(grad_unit.astype(jnp.bfloat16), "dp").astype(jnp.float32)
    new_w, new_v = update_tiles(grad_sum, centers, w_unit, w_norm, momentum, live_tile)
    return (loss, embed_grad, new_w, new_v)


DIGIT_ROWS = 8
ON_CHIP_BYTES = 24 << 20
KERNEL_VMEM = 24 << 20
DEAD_BIAS = -1e30
VMEM_SPEC = pl.BlockSpec(memory_space=pltpu.VMEM)
SMEM_SPEC = pl.BlockSpec(memory_space=pltpu.SMEM)


def call(kernel, outs, in_specs, scratch=(), flops=0, moved=0):
    return pl.pallas_call(
        kernel,
        out_shape=outs,
        in_specs=in_specs,
        out_specs=jax.tree.map(lambda _: VMEM_SPEC, outs),
        scratch_shapes=scratch,
        compiler_params=pltpu.CompilerParams(vmem_limit_bytes=KERNEL_VMEM),
        cost_estimate=pl.CostEstimate(flops=flops, bytes_accessed=moved, transcendentals=0),
    )


def unit_scale(values):
    return lax.rsqrt(jnp.sum(values * values, axis=-1, keepdims=True) + tiny_eps)


def pack_kernel(x_ref, label_ref, out_ref):
    rows_dev, width = x_ref.shape
    out_ref[0:rows_dev, :] = x_ref[...]
    label = label_ref[...]
    digit_row = lax.broadcasted_iota(jnp.int32, (DIGIT_ROWS, rows_dev), 0)
    digits = jnp.where(digit_row < 4, (label >> (8 * jnp.minimum(digit_row, 3))) & 255, 0)
    out_ref[rows_dev:, :] = jnp.zeros((DIGIT_ROWS, width), jnp.bfloat16)
    out_ref[rows_dev:, 0:rows_dev] = digits.astype(jnp.float32).astype(jnp.bfloat16)


def unit_centers_kernel(centers_ref, unit_ref):
    def step(slot, carry):
        w_float = centers_ref[slot].astype(jnp.float32)
        w_unit = (w_float * unit_scale(w_float)).astype(jnp.bfloat16)
        unit_ref[slot] = w_unit * jnp.bfloat16(logit_scale)
        return carry

    lax.fori_loop(0, centers_ref.shape[0], step, 0)


def logits_kernel(
    z_count, rows_dev, chunk, counts_ref, blocks_ref, source_ref, w_ref,
    x_ref, exp_ref, stat_ref, target_ref, digit_ref,
):
    z_own = lax.axis_index("center") // 2
    piece_rows = rows_dev + DIGIT_ROWS
    pieces = source_ref.shape[0] // piece_rows
    batch, width = x_ref.shape
    slots = blocks_ref.shape[0]
    flat = w_ref.shape[0]
    blk_size = flat // slots
    for piece in range(pieces):
        group, z_rel = divmod(piece, z_count)
        place = group * z_count + (z_own ^ z_rel)
        base = piece * piece_rows
        x_float = source_ref[base : base + rows_dev, :].astype(jnp.float32)
        start = pl.multiple_of(place * rows_dev, rows_dev)
        x_ref[pl.ds(start, rows_dev), :] = (x_float * unit_scale(x_float)).astype(jnp.bfloat16)
        digit_ref[place] = source_ref[base + rows_dev : base + piece_rows, :128].astype(jnp.float32)
    digits = digit_ref[...].reshape(pieces * DIGIT_ROWS, 128).astype(jnp.bfloat16)
    lane = lax.broadcasted_iota(jnp.int32, (128, batch), 0)
    column = lax.broadcasted_iota(jnp.int32, (128, batch), 1)
    spread = jnp.where(column % rows_dev == lane, 1.0, 0.0).astype(jnp.bfloat16)
    spread_digits = jnp.dot(digits, spread, preferred_element_type=jnp.float32)
    spread_digits = spread_digits.reshape(pieces, DIGIT_ROWS, batch)
    owner = lax.broadcasted_iota(jnp.int32, (DIGIT_ROWS, batch), 1) // rows_dev
    digit_rows = jnp.zeros((DIGIT_ROWS, batch), jnp.float32)
    for place in range(pieces):
        digit_rows = digit_rows + jnp.where(owner == place, spread_digits[place], 0.0)
    digit_ints = digit_rows.astype(jnp.int32)
    label = digit_ints[0:1] + 256 * (digit_ints[1:2] + 256 * (digit_ints[2:3] + 256 * digit_ints[3:4]))
    label_block, label_col = label // blk_size, label % blk_size
    target = jnp.full((1, batch), -1, jnp.int32)
    for slot in range(slots):
        target = jnp.where(label_block == blocks_ref[slot], slot * blk_size + label_col, target)
    target_ref[...] = target
    live_rows = counts_ref[0] * blk_size

    def step(index, carry):
        total, positive = carry
        first = pl.multiple_of(index * chunk, chunk)
        logit = lax.dot_general(
            w_ref[pl.ds(first, chunk), :], x_ref[...], (((1,), (1,)), ((), ())),
            preferred_element_type=jnp.float32,
        )
        row = lax.broadcasted_iota(jnp.int32, (chunk, batch), 0)
        row_one = lax.broadcasted_iota(jnp.int32, (chunk, 1), 0) + first
        bias = jnp.where(row_one < live_rows, 0.0, DEAD_BIAS)
        hit = row == target - first
        logit = jnp.where(hit, logit - logit_scale * margin_cos, logit)
        exp_z = jnp.exp(logit + bias)
        exp_ref[pl.ds(first, chunk), :] = exp_z
        positive = positive + jnp.sum(jnp.where(hit, logit, 0.0).reshape(chunk // 8, 8, batch), axis=0)
        total = total + jnp.sum(exp_z.reshape(chunk // 8, 8, batch), axis=0)
        return total, positive

    zeros = jnp.zeros((8, batch), jnp.float32)
    total, positive = lax.fori_loop(0, flat // chunk, step, (zeros, zeros))
    stat_ref[0:1, :] = jnp.sum(total, axis=0, keepdims=True)
    stat_ref[1:2, :] = jnp.sum(positive, axis=0, keepdims=True)


def error_rows(exp_z, first, scale, target):
    row = lax.broadcasted_iota(jnp.int32, exp_z.shape, 0)
    scaled = exp_z * scale
    return jnp.where(row == target - first, scaled - 1.0, scaled).astype(jnp.bfloat16)


def embed_kernel(
    z_count, chunk, exp_ref, pair_exp_ref, stat_ref, target_ref, pair_target_ref, w_ref,
    keep_ref, send_ref, sum_ref, pair_sum_ref,
):
    z_own = lax.axis_index("center") // 2
    rows = sum_ref.shape[0]
    rows_dev = rows // z_count
    half = stat_ref.shape[1] // 2
    sides = (
        (exp_ref, target_ref, 0, sum_ref, keep_ref),
        (pair_exp_ref, pair_target_ref, half, pair_sum_ref, send_ref),
    )
    for _, _, _, total_ref, _ in sides:
        total_ref[...] = jnp.zeros_like(total_ref)

    def step(index, carry):
        first = pl.multiple_of(index * chunk, chunk)
        for values_ref, hits_ref, offset, total_ref, _ in sides:
            scale = 1.0 / stat_ref[0:1, offset : offset + rows]
            err = error_rows(values_ref[pl.ds(first, chunk), :rows], first, scale, hits_ref[0:1, :rows])
            total_ref[...] += lax.dot_general(
                err, w_ref[pl.ds(first, chunk), :], (((0,), (0,)), ((), ())),
                preferred_element_type=jnp.float32,
            )
        return carry

    lax.fori_loop(0, exp_ref.shape[0] // chunk, step, 0)
    for _, _, _, total_ref, out_ref in sides:
        for z_to in range(z_count):
            out_ref[z_own ^ z_to] = total_ref[z_to * rows_dev : (z_to + 1) * rows_dev, :]


def update_kernel(
    counts_ref, exp_ref, pair_exp_ref, stat_ref, target_ref, pair_target_ref, x_ref, pair_x_ref,
    centers_ref, momentum_ref, new_w_ref, new_v_ref,
):
    step_slots, blk_size, width = centers_ref.shape
    rows = step_slots * blk_size
    first = pl.multiple_of(pl.program_id(0) * rows, rows)
    half = stat_ref.shape[1] // 2
    grad_unit = jnp.zeros((rows, width), jnp.float32)
    for side, (values_ref, hits_ref, units_ref) in enumerate(
        ((exp_ref, target_ref, x_ref), (pair_exp_ref, pair_target_ref, pair_x_ref))
    ):
        scale = 1.0 / stat_ref[0:1, side * half : (side + 1) * half]
        err = error_rows(values_ref[pl.ds(first, rows), :], first, scale, hits_ref[...])
        grad_unit = grad_unit + jnp.dot(err, units_ref[...], preferred_element_type=jnp.float32)
    grad_unit = grad_unit * logit_scale
    w_float = centers_ref[...].reshape(rows, width).astype(jnp.float32)
    inverse = unit_scale(w_float)
    w_unit = w_float * inverse
    along = jnp.sum(w_unit * grad_unit, axis=-1, keepdims=True)
    grad_w = (grad_unit - w_unit * along) * inverse
    momentum = momentum_ref[...].reshape(rows, width)
    row = lax.broadcasted_iota(jnp.int32, (rows, 1), 0) + first
    live = row < counts_ref[0] * blk_size
    new_v = jnp.where(live, momentum_rate * momentum + grad_w, momentum)
    new_w = jnp.where(live, w_float - learn_rate * new_v, w_float)
    new_v_ref[...] = new_v.reshape(new_v_ref.shape)
    new_w_ref[...] = new_w.astype(jnp.bfloat16).reshape(new_w_ref.shape)


def finish_kernel(z_count, packed_ref, keep_ref, stat_ref, *refs):
    *grad_refs, loss_ref, grad_ref = refs
    z_own = lax.axis_index("center") // 2
    rows_dev, width = grad_ref.shape
    grad_x = keep_ref[0]
    for received in grad_refs:
        grad_x = grad_x + received[...].astype(jnp.float32)
    x_float = packed_ref[0:rows_dev, :].astype(jnp.float32)
    inverse = unit_scale(x_float)
    x_unit = x_float * inverse
    along = jnp.sum(x_unit * grad_x, axis=-1, keepdims=True)
    grad_ref[...] = (grad_x - x_unit * along) * inverse
    loss = jnp.log(stat_ref[0:1, : z_count * rows_dev]) - stat_ref[1:2, : z_count * rows_dev]
    own = jnp.zeros((1, rows_dev), jnp.float32)
    for z_at in range(z_count):
        own = jnp.where(z_own == z_at, loss[:, z_at * rows_dev : (z_at + 1) * rows_dev], own)
    loss_ref[...] = own


def on_device_permutes(groups, z_count, embeddings, labels, centers, momentum, block_list, counts):
    rows_dev, width = embeddings.shape
    slots, blk_size, _ = centers.shape
    flat = slots * blk_size
    cores = z_count * 2
    half = groups * z_count * rows_dev
    chunk = 2 * blk_size
    axes = ("dp", "center")
    shape = jax.ShapeDtypeStruct

    def exchange(array, group_mask, center_mask):
        pairs = [
            (group * cores + center, (group ^ group_mask) * cores + (center ^ center_mask))
            for group in range(groups)
            for center in range(cores)
        ]
        return lax.ppermute(array, axes, pairs)

    packed = call(
        pack_kernel, shape((rows_dev + DIGIT_ROWS, width), jnp.bfloat16), [VMEM_SPEC] * 2
    )(embeddings, labels.reshape(1, rows_dev))
    column = jnp.concatenate(
        [packed] + [exchange(packed, 0, 2 * mask) for mask in range(1, z_count)], axis=0
    )
    mine = jnp.concatenate(
        [column] + [exchange(column, mask, 0) for mask in range(1, groups)], axis=0
    )
    pair = exchange(mine, 0, 1)
    w_bf = call(
        unit_centers_kernel,
        shape((slots, blk_size, width), jnp.bfloat16),
        [VMEM_SPEC],
        flops=4 * flat * width,
        moved=4 * flat * width,
    )(centers).reshape(flat, width)
    logits = call(
        functools.partial(logits_kernel, z_count, rows_dev, chunk),
        (
            shape((half, width), jnp.bfloat16),
            shape((flat, half), jnp.float32),
            shape((2, half), jnp.float32),
            shape((1, half), jnp.int32),
        ),
        [SMEM_SPEC, SMEM_SPEC, VMEM_SPEC, VMEM_SPEC],
        [pltpu.VMEM((groups * z_count, DIGIT_ROWS, 128), jnp.float32)],
        flops=2 * flat * width * half,
        moved=4 * flat * half,
    )
    x_bf, exp_z, stats, target = logits(counts, block_list, mine, w_bf)
    pair_x, pair_exp, pair_stats, pair_target = logits(counts, block_list, pair, w_bf)
    swapped = exchange(jnp.concatenate([pair_stats, stats], axis=1), 0, 1)
    stats = jnp.concatenate([stats, pair_stats], axis=1) + swapped
    for bit in range(z_count.bit_length() - 1):
        stats = stats + exchange(stats, 0, 2 << bit)
    keep, send = call(
        functools.partial(embed_kernel, z_count, chunk),
        (shape((z_count, rows_dev, width), jnp.float32),) * 2,
        [VMEM_SPEC] * 6,
        [pltpu.VMEM((z_count * rows_dev, width), jnp.float32)] * 2,
        flops=4 * flat * width * z_count * rows_dev,
        moved=8 * flat * z_count * rows_dev,
    )(exp_z, pair_exp, stats, target, pair_target, w_bf)
    keep = keep + exchange(send, 0, 1)
    sent = keep.astype(jnp.bfloat16)
    received = [exchange(sent[mask], 0, 2 * mask) for mask in range(1, z_count)]
    step_slots = math.gcd(slots, 2)
    tile = pl.BlockSpec((step_slots, blk_size, width), lambda step: (step, 0, 0))
    new_w, new_v = pl.pallas_call(
        update_kernel,
        grid=(slots // step_slots,),
        out_shape=(shape(centers.shape, centers.dtype), shape(momentum.shape, momentum.dtype)),
        in_specs=[SMEM_SPEC] + [VMEM_SPEC] * 7 + [tile, tile],
        out_specs=(tile, tile),
        compiler_params=pltpu.CompilerParams(vmem_limit_bytes=KERNEL_VMEM),
        cost_estimate=pl.CostEstimate(
            flops=4 * flat * width * half, bytes_accessed=12 * flat * width, transcendentals=0
        ),
    )(counts, exp_z, pair_exp, stats, target, pair_target, x_bf, pair_x, centers, momentum)
    loss, embed_grad = call(
        functools.partial(finish_kernel, z_count),
        (shape((1, rows_dev), jnp.float32), shape((rows_dev, width), jnp.float32)),
        [VMEM_SPEC] * (3 + len(received)),
    )(packed, keep, stats, *received)
    return (loss.reshape(rows_dev), embed_grad, new_w, new_v)


def solution(mesh):
    groups, cores = mesh.shape["dp"], mesh.shape["center"]

    def on_mesh(embeddings, labels, centers, momentum, block_list, counts):
        batch, width = embeddings.shape
        tiles, blk_size, _ = centers.shape
        rows_dev = batch // (groups * cores)
        flat = tiles // cores * blk_size
        powers = groups & (groups - 1) == 0 and cores & (cores - 1) == 0 and cores >= 4
        fits = 4 * flat * batch + 8 * batch * width <= ON_CHIP_BYTES
        shapes = rows_dev == 32 and width % 128 == 0 and blk_size == 128
        whole = (cores // 2 * rows_dev) % 128 == 0
        body = on_device
        if powers and fits and shapes and whole:
            body = functools.partial(on_device_permutes, groups, cores // 2)
        return jax.shard_map(
            body,
            mesh=mesh,
            in_specs=(
                P(("dp", "center"), None),
                P(("dp", "center")),
                P("center", None, None),
                P("center", None, None),
                P("center"),
                P("center"),
            ),
            out_specs=(
                P(("dp", "center")),
                P(("dp", "center"), None),
                P("center", None, None),
                P("center", None, None),
            ),
            check_vma=False,
        )(embeddings, labels, centers, momentum, block_list, counts)

    return on_mesh
```
